256 devices in a mesh: orb: 8 (over x, core), dom: 32 (over y, z).
Axes of the slice: x: 4, y: 4, z: 8, core: 2. Of those that a mesh axis runs over, the one named last changes fastest.
Arguments:
- orbitals: float32 [768, 128, 8, 128], P('orb', 'dom'), may hold values from -6 to 6
- potential: float32 [128, 8, 128], P('dom'), may hold values from -1 to 3
- prev_gradient: float32 [768, 128, 8, 128], P('orb', 'dom'), may hold values from -24 to 24
- prev_direction: float32 [768, 128, 8, 128], P('orb', 'dom'), may hold values from -24 to 24
Outputs:
- new_orbitals: float32 [768, 128, 8, 128], P('orb', 'dom')
- new_direction: float32 [768, 128, 8, 128], P('orb', 'dom')
- gradient: float32 [768, 128, 8, 128], P('orb', 'dom')
The draws below stay inside these ranges and needn't reach their ends.
All inputs are finite; a program needn't handle non-finite values.
Results may differ from the reference program's by a relative error of at most 0.0002.
Values sent between devices are 32-bit elements; how exact they have to be, the bound alone decides.
No kernel may reach another device: no remote copies, remote signals or barrier semaphores. Data moves between devices by JAX's collectives and lax.ppermute only.
A program may use at most 128 MiB of HBM per device.

```python
import jax
import jax.numpy as jnp
from jax import lax

NORB = 768
NX = 128
NY = 8
NZ = 128


def block_levels(rng, extent, shards, smallest, largest):
    factor_of = 1.0
    for position, shards_of in shards:
        heights = jax.random.uniform(jax.random.fold_in(jax.random.fold_in(rng, 6), position), (shards_of,), jnp.float32, smallest / len(shards), largest / len(shards))
        factor_of = factor_of * jnp.repeat(jnp.exp(heights), extent[position] // shards_of).reshape((-1,) + (1,) * (len(extent) - 1 - position))
    return factor_of


def scatter_about(stream_key, dims, scale, reach, cuts=(), dtype=jnp.bfloat16):
    values = scale * jax.random.normal(stream_key, dims, jnp.float32)
    if cuts:
        values = values * block_levels(stream_key, dims, cuts, -0.22, 0.18)
    return jnp.clip(values, -reach, reach).astype(dtype)


def setup_inputs(seed: int = 0) -> dict:
    key_of = jax.random.split(jax.random.key(seed), 5)
    return {
        "orbitals": scatter_about(key_of[0], (NORB, NZ, NY, NX), 1.0, 6.0, ((0, 8), (1, 32)), jnp.float32),
        "potential": jnp.clip(-1.0 + 4.0 * jax.random.uniform(key_of[1], (NZ, NY, NX), jnp.float32) ** block_levels(key_of[1], (NZ, NY, NX), ((0, 32),), -0.2, 0.2), -1.0, 3.0),
        "prev_gradient": scatter_about(key_of[2], (NORB, NZ, NY, NX), 4.0, 24.0, ((0, 8), (1, 32)), jnp.float32),
        "prev_direction": scatter_about(key_of[3], (NORB, NZ, NY, NX), 4.0, 24.0, ((0, 8), (1, 32)), jnp.float32),
    }


coeffs = (-205.0 / 72.0, 8.0 / 5.0, -1.0 / 5.0, 8.0 / 315.0, -1.0 / 560.0)
step_length = 0.05


def laplace(padded, planes, lines, columns):
    center = padded[:, 4:4 + planes, 4:4 + lines, 4:4 + columns]
    total = 3.0 * coeffs[0] * center
    for offset in range(1, 5):
        total = total + coeffs[offset] * (padded[:, 4 + offset:4 + offset + planes, 4:4 + lines, 4:4 + columns] + padded[:, 4 - offset:4 - offset + planes, 4:4 + lines, 4:4 + columns])
        total = total + coeffs[offset] * (padded[:, 4:4 + planes, 4 + offset:4 + offset + lines, 4:4 + columns] + padded[:, 4:4 + planes, 4 - offset:4 - offset + lines, 4:4 + columns])
        total = total + coeffs[offset] * (padded[:, 4:4 + planes, 4:4 + lines, 4 + offset:4 + offset + columns] + padded[:, 4:4 + planes, 4:4 + lines, 4 - offset:4 - offset + columns])
    return total


def highdot(left, right):
    return jnp.dot(left, right, precision=lax.Precision.HIGHEST, preferred_element_type=jnp.float32)


def reference(orbitals, potential, prev_gradient, prev_direction):
    count = orbitals.shape[0]
    padded = jnp.pad(orbitals, ((0, 0), (4, 4), (4, 4), (4, 4)))
    lap = laplace(padded, orbitals.shape[1], orbitals.shape[2], orbitals.shape[3])
    image = -0.5 * lap + potential[None] * orbitals
    cmat = orbitals.reshape(count, -1)
    hmat_rows = image.reshape(count, -1)
    cells = cmat.shape[1]
    correlation = highdot(cmat, cmat.T) / cells
    hamilton = highdot(cmat, hmat_rows.T) / cells
    grad = 4.0 * hmat_rows - 2.0 * highdot(correlation.T, hmat_rows) - 2.0 * highdot(hamilton.T, cmat)
    grad = grad.reshape(orbitals.shape)
    both = jnp.sum(grad * grad)
    cross = jnp.sum(grad * prev_gradient)
    before = jnp.sum(prev_gradient * prev_gradient)
    beta = (both - cross) / before
    direction = -grad + beta * prev_direction
    return orbitals + step_length * direction, direction, grad
```

```python
import jax
import jax.numpy as jnp
from jax import lax
from jax.experimental import pallas as pl
from jax.experimental.pallas import tpu as pltpu
from jax.sharding import PartitionSpec as P

coeffs = (-205.0 / 72.0, 8.0 / 5.0, -1.0 / 5.0, 8.0 / 315.0, -1.0 / 560.0)
step_length = 0.05
ZS = 8


def shift_orb(v, k):
    n = lax.axis_size("orb")
    return lax.ppermute(v, "orb", [(i, (i + k) % n) for i in range(n)])


def swap_core(v):
    n = lax.axis_size("orb")
    return lax.ppermute(v, "orb", [(i, i ^ 1) for i in range(n)])


def shift_z(v, k):
    n = lax.axis_size("dom")
    return lax.ppermute(v, "dom", [(i, (i // ZS) * ZS + (i + k) % ZS) for i in range(n)])


def shift_y(v, k):
    n = lax.axis_size("dom")
    return lax.ppermute(v, "dom", [(i, (i + k * ZS) % n) for i in range(n)])


def gather_orbitals(own):
    half = own.shape[0] // 2
    right, left = shift_orb(own, 2), shift_orb(own, -2)
    mate = swap_core(own)
    far_a, far_b = shift_orb(right[:half], 2), shift_orb(left[half:], -2)
    mate_right, mate_left = swap_core(right), swap_core(left)
    mate_a, mate_b = swap_core(far_a), swap_core(far_b)
    return [own, mate, right, left, mate_right, mate_left], [far_a, far_b, mate_a, mate_b]


def stencil_kernel(c_ref, l_ref, r_ref, v_ref, o_ref):
    rows = c_ref.shape[0]
    lane = lax.broadcasted_iota(jnp.int32, (rows, 128), 1)

    def tile(ref, plane, line):
        start = (plane * 8 + line) * 128
        return ref[:, start : start + 128]

    def plane_tile(plane, line):
        if plane < 0:
            return tile(l_ref, plane + 4, line)
        if plane > 3:
            return tile(r_ref, plane - 4, line)
        return tile(c_ref, plane, line)

    for plane in range(4):
        for line in range(8):
            start = (plane * 8 + line) * 128
            center = tile(c_ref, plane, line)
            total = (v_ref[:, start : start + 128] - 1.5 * coeffs[0]) * center
            for k in range(1, 5):
                near = plane_tile(plane + k, line) + plane_tile(plane - k, line)
                if line + k < 8:
                    near = near + tile(c_ref, plane, line + k)
                if line - k >= 0:
                    near = near + tile(c_ref, plane, line - k)
                near = near + jnp.where(lane < 128 - k, pltpu.roll(center, 128 - k, 1), 0.0)
                near = near + jnp.where(lane >= k, pltpu.roll(center, k, 1), 0.0)
                total = total + (-0.5 * coeffs[k]) * near
            o_ref[:, start : start + 128] = total


def apply_hamiltonian(c, left, right, pot):
    rows, cells = c.shape
    step = 8
    block = pl.BlockSpec((step, cells), lambda i: (i, 0))
    return pl.pallas_call(
        stencil_kernel,
        out_shape=jax.ShapeDtypeStruct(c.shape, jnp.float32),
        grid=(rows // step,),
        in_specs=[block, block, block, pl.BlockSpec((1, cells), lambda i: (0, 0))],
        out_specs=block,
        cost_estimate=pl.CostEstimate(flops=40 * rows * cells, bytes_accessed=16 * rows * cells, transcendentals=0),
        name="hamiltonian",
    )(c, left, right, pot)


def split(v):
    hi = v.astype(jnp.bfloat16)
    return hi, (v - hi.astype(jnp.float32)).astype(jnp.bfloat16)


def dot_nt(a, b):
    return lax.dot_general(a, b, (((1,), (1,)), ((), ())), preferred_element_type=jnp.float32)


def gram(c, image, blocks):
    own, cells = c.shape
    sizes = [b.shape[0] for b in blocks]
    total = sum(sizes)
    chunk = 512

    def kernel(c_ref, h_ref, *rest):
        refs, o_ref, hi_ref, lo_ref, w_ref = rest[: len(sizes)], rest[-4], rest[-3], rest[-2], rest[-1]
        at = 0
        for ref, size in zip(refs, sizes):
            hi, lo = split(ref[...])
            hi_ref[at : at + size, :] = hi
            lo_ref[at : at + size, :] = lo
            at += size
        c_hi, c_lo = split(c_ref[...])
        h_hi, h_lo = split(h_ref[...])
        w_ref[0:own, :] = c_hi
        w_ref[own : 2 * own, :] = h_hi
        w_ref[2 * own : 3 * own, :] = c_lo
        w_ref[3 * own : 4 * own, :] = h_lo
        with_hi = dot_nt(w_ref[...], hi_ref[...])
        part = with_hi[: 2 * own] + with_hi[2 * own :] + dot_nt(w_ref[0 : 2 * own, :], lo_ref[...])

        @pl.when(pl.program_id(0) == 0)
        def _():
            o_ref[...] = part

        @pl.when(pl.program_id(0) > 0)
        def _():
            o_ref[...] += part

    return pl.pallas_call(
        kernel,
        out_shape=jax.ShapeDtypeStruct((2 * own, total), jnp.float32),
        grid=(cells // chunk,),
        in_specs=[pl.BlockSpec((s, chunk), lambda i: (0, i)) for s in [own, own] + sizes],
        out_specs=pl.BlockSpec((2 * own, total), lambda i: (0, 0)),
        scratch_shapes=[
            pltpu.VMEM((total, chunk), jnp.bfloat16),
            pltpu.VMEM((total, chunk), jnp.bfloat16),
            pltpu.VMEM((4 * own, chunk), jnp.bfloat16),
        ],
        cost_estimate=pl.CostEstimate(
            flops=12 * own * total * cells, bytes_accessed=4 * cells * (2 * own + total), transcendentals=0
        ),
        name="gram",
    )(c, image, *blocks)


def sum_over_slabs(part):
    rows, columns = part.shape
    chunk = rows // ZS
    z = lax.rem(lax.axis_index("dom"), ZS)
    pieces = part.reshape(ZS, chunk, columns)

    def piece(k):
        return lax.dynamic_index_in_dim(pieces, lax.rem(z + k, ZS), 0, keepdims=False)

    total = piece(0)
    for got in [shift_z(piece(k), k) for k in range(1, ZS)]:
        total = total + got
    count = lax.axis_size("dom") // ZS
    for got in [shift_y(total, k) for k in range(1, count)]:
        total = total + got
    out = jnp.zeros_like(pieces)
    out = lax.dynamic_update_slice_in_dim(out, total[None], z, 0)
    for k in range(1, ZS):
        out = lax.dynamic_update_slice_in_dim(out, shift_z(total, k)[None], lax.rem(z - k + ZS, ZS), 0)
    return out.reshape(rows, columns)


def gradient_of(overlap, blocks, images, own_image, prev, cells_total):
    own, cells = own_image.shape
    sizes = [b.shape[0] for b in blocks]
    total = sum(sizes)
    count = len(sizes)
    chunk = 512

    def kernel(s_ref, hc_ref, p_ref, *rest):
        c_refs, i_refs = rest[:count], rest[count : 2 * count]
        g_ref, sums_ref, w_hi, w_lo, hi_ref, lo_ref = rest[2 * count :]

        @pl.when(pl.program_id(0) == 0)
        def _():
            for index in range(2):
                hi, lo = split(s_ref[(1 - index) * own : (2 - index) * own, :] * (-2.0 / cells_total))
                w_hi[:own, index * total : (index + 1) * total] = hi
                w_hi[own:, index * total : (index + 1) * total] = lo
            sums_ref[...] = jnp.zeros_like(sums_ref)

        at = 0
        for ref, size in zip(c_refs + i_refs, sizes + sizes):
            hi, lo = split(ref[...])
            hi_ref[at : at + size, :] = hi
            lo_ref[at : at + size, :] = lo
            at += size
        with_hi = jnp.dot(w_hi[...], hi_ref[...], preferred_element_type=jnp.float32)
        grad = with_hi[:own] + with_hi[own:]
        grad = grad + jnp.dot(w_hi[:own, :], lo_ref[...], preferred_element_type=jnp.float32)
        grad = grad + 4.0 * hc_ref[...]
        g_ref[...] = grad
        prev_block = p_ref[...]

        def folded(v):
            v = v.reshape(own // 8, 8, chunk).sum(0)
            return sum(v[:, k * 128 : (k + 1) * 128] for k in range(chunk // 128))

        sums_ref[0:8, :] += folded(grad * grad)
        sums_ref[8:16, :] += folded(grad * prev_block)
        sums_ref[16:24, :] += folded(prev_block * prev_block)

    column = [pl.BlockSpec((s, chunk), lambda i: (0, i)) for s in sizes]
    own_block = pl.BlockSpec((own, chunk), lambda i: (0, i))
    return pl.pallas_call(
        kernel,
        out_shape=(
            jax.ShapeDtypeStruct((own, cells), jnp.float32),
            jax.ShapeDtypeStruct((24, 128), jnp.float32),
        ),
        grid=(cells // chunk,),
        in_specs=[pl.BlockSpec((2 * own, total), lambda i: (0, 0)), own_block, own_block] + column + column,
        out_specs=(own_block, pl.BlockSpec((24, 128), lambda i: (0, 0))),
        scratch_shapes=[
            pltpu.VMEM((2 * own, 2 * total), jnp.bfloat16),
            pltpu.VMEM((8, 128), jnp.bfloat16),
            pltpu.VMEM((2 * total, chunk), jnp.bfloat16),
            pltpu.VMEM((2 * total, chunk), jnp.bfloat16),
        ],
        cost_estimate=pl.CostEstimate(
            flops=12 * own * total * cells, bytes_accessed=8 * cells * total, transcendentals=0
        ),
        name="gradient",
    )(overlap, own_image, prev, *blocks, *images)


def on_device(orbitals, potential, prev_gradient, prev_direction):
    own = orbitals.shape[0]
    slabs = lax.axis_size("dom")
    c = orbitals.reshape(own, -1)
    left = lax.ppermute(c, "dom", [(i, i + 1) for i in range(slabs - 1)])
    right = lax.ppermute(c, "dom", [(i + 1, i) for i in range(slabs - 1)])
    near, far = gather_orbitals(c)
    image = apply_hamiltonian(c, left, right, potential.reshape(1, -1))
    near_image, far_image = gather_orbitals(image)
    part = jnp.concatenate([gram(c, image, near), gram(c, image, far)], axis=1)
    overlap = sum_over_slabs(part)
    grad, sums = gradient_of(
        overlap, near + far, near_image + far_image, image, prev_gradient.reshape(own, -1), slabs * c.shape[1]
    )
    devices = lax.axis_size("orb") * slabs
    sums = sums.reshape(3, 8, 128).sum(axis=(1, 2))
    sums = jnp.broadcast_to(jnp.pad(sums, (0, 125))[None], (devices, 128))
    sums = lax.all_to_all(sums, ("orb", "dom"), split_axis=0, concat_axis=0, tiled=True)
    sums = sums.sum(axis=0)
    beta = (sums[0] - sums[1]) / sums[2]
    grad = grad.reshape(orbitals.shape)
    direction = -grad + beta * prev_direction
    return (orbitals + step_length * direction, direction, grad)


def solution(mesh):
    in_specs = (
        P("orb", "dom", None, None),
        P("dom", None, None),
        P("orb", "dom", None, None),
        P("orb", "dom", None, None),
    )
    out_specs = (
        P("orb", "dom", None, None),
        P("orb", "dom", None, None),
        P("orb", "dom", None, None),
    )
    return jax.shard_map(
        on_device, mesh=mesh, in_specs=in_specs, out_specs=out_specs, check_vma=False
    )
```

```python
import jax
import jax.numpy as jnp
from jax import lax
from jax.experimental import pallas as pl
from jax.experimental.pallas import tpu as pltpu
from jax.sharding import PartitionSpec as P

coeffs = (-205.0 / 72.0, 8.0 / 5.0, -1.0 / 5.0, 8.0 / 315.0, -1.0 / 560.0)
step_length = 0.05
VMEM_LIMIT = 32 * 1024 * 1024
ZS = 8


def shift_orb(v, k):
    n = lax.axis_size("orb")
    return lax.ppermute(v, "orb", [(i, (i + k) % n) for i in range(n)])


def swap_core(v):
    n = lax.axis_size("orb")
    return lax.ppermute(v, "orb", [(i, i ^ 1) for i in range(n)])


def flip_z(v, k):
    n = lax.axis_size("dom")
    return lax.ppermute(v, "dom", [(i, i ^ k) for i in range(n)])


def shift_y(v, k):
    n = lax.axis_size("dom")
    return lax.ppermute(v, "dom", [(i, (i + k * ZS) % n) for i in range(n)])


def gather_near(first, second):
    right1, left2 = shift_orb(first, 2), shift_orb(second, -2)
    right2, left1 = shift_orb(second, 2), shift_orb(first, -2)
    blocks = [first, second, right1, left2, right2, left1]
    return blocks + [swap_core(b) for b in blocks]


def gather_far(near):
    far1, far2 = shift_orb(near[2], 2), shift_orb(near[3], -2)
    return [far1, far2, swap_core(far1), swap_core(far2)]


def stencil_kernel(c_ref, l_ref, r_ref, v_ref, o_ref):
    lane = lax.broadcasted_iota(jnp.int32, (8, 128), 1)

    @pl.loop(0, c_ref.shape[0] // 8)
    def _(group):
        rows = pl.ds(pl.multiple_of(group * 8, 8), 8)

        def tile(ref, plane, line):
            start = (plane * 8 + line) * 128
            return ref[rows, start : start + 128]

        def plane_tile(plane, line):
            if plane < 0:
                return tile(l_ref, plane + 4, line)
            if plane > 3:
                return tile(r_ref, plane - 4, line)
            return tile(c_ref, plane, line)

        for plane in range(4):
            for line in range(8):
                start = (plane * 8 + line) * 128
                center = tile(c_ref, plane, line)
                total = (v_ref[:, start : start + 128] - 1.5 * coeffs[0]) * center
                for k in range(1, 5):
                    near = plane_tile(plane + k, line) + plane_tile(plane - k, line)
                    if line + k < 8:
                        near = near + tile(c_ref, plane, line + k)
                    if line - k >= 0:
                        near = near + tile(c_ref, plane, line - k)
                    near = near + jnp.where(lane < 128 - k, pltpu.roll(center, 128 - k, 1), 0.0)
                    near = near + jnp.where(lane >= k, pltpu.roll(center, k, 1), 0.0)
                    total = total + (-0.5 * coeffs[k]) * near
                o_ref[rows, start : start + 128] = total


def apply_hamiltonian(c, left, right, pot):
    rows, cells = c.shape
    step = 24
    block = pl.BlockSpec((step, cells), lambda i: (i, 0))
    return pl.pallas_call(
        stencil_kernel,
        out_shape=jax.ShapeDtypeStruct(c.shape, jnp.float32),
        grid=(rows // step,),
        in_specs=[block, block, block, pl.BlockSpec((1, cells), lambda i: (0, 0))],
        out_specs=block,
        cost_estimate=pl.CostEstimate(flops=40 * rows * cells, bytes_accessed=16 * rows * cells, transcendentals=0),
        name="hamiltonian",
    )(c, left, right, pot)


def split(v):
    hi = v.astype(jnp.bfloat16)
    return hi, (v - hi.astype(jnp.float32)).astype(jnp.bfloat16)


def dot_nt(a, b):
    return lax.dot_general(a, b, (((1,), (1,)), ((), ())), preferred_element_type=jnp.float32)


def store_split(refs, hi_ref, lo_ref):
    at = 0
    for ref in refs:
        hi, lo = split(ref[...])
        hi_ref[at : at + ref.shape[0], :] = hi
        lo_ref[at : at + ref.shape[0], :] = lo
        at += ref.shape[0]


def gram(own_blocks, blocks):
    cells = blocks[0].shape[1]
    count = len(own_blocks)
    rows = sum(b.shape[0] for b in own_blocks)
    total = sum(b.shape[0] for b in blocks)
    chunk = 1024

    def kernel(*rest):
        o_ref, hi_ref, lo_ref, w_ref = rest[-4:]
        store_split(rest[count:-4], hi_ref, lo_ref)
        store_split(rest[:count], w_ref.at[0:rows], w_ref.at[rows : 2 * rows])
        with_hi = dot_nt(w_ref[...], hi_ref[...])
        part = with_hi[:rows] + with_hi[rows:] + dot_nt(w_ref[0:rows, :], lo_ref[...])

        @pl.when(pl.program_id(0) == 0)
        def _():
            o_ref[...] = part

        @pl.when(pl.program_id(0) > 0)
        def _():
            o_ref[...] += part

    return pl.pallas_call(
        kernel,
        out_shape=jax.ShapeDtypeStruct((rows, total), jnp.float32),
        grid=(cells // chunk,),
        in_specs=[pl.BlockSpec((b.shape[0], chunk), lambda i: (0, i)) for b in own_blocks + blocks],
        out_specs=pl.BlockSpec((rows, total), lambda i: (0, 0)),
        scratch_shapes=[
            pltpu.VMEM((total, chunk), jnp.bfloat16),
            pltpu.VMEM((total, chunk), jnp.bfloat16),
            pltpu.VMEM((2 * rows, chunk), jnp.bfloat16),
        ],
        compiler_params=pltpu.CompilerParams(vmem_limit_bytes=VMEM_LIMIT),
        cost_estimate=pl.CostEstimate(
            flops=6 * rows * total * cells, bytes_accessed=4 * cells * (rows + total), transcendentals=0
        ),
        name="gram",
    )(*own_blocks, *blocks)


def sum_over_slabs(part):
    rows, columns = part.shape
    quad = ZS // 2
    z = lax.rem(lax.axis_index("dom"), ZS)
    high, low = z // quad, lax.rem(z, quad)
    pieces = part.reshape(2, quad, rows // ZS, columns)

    def piece(k):
        return lax.dynamic_index_in_dim(pieces, low ^ k, 1, keepdims=False)

    total = piece(0)
    for got in [flip_z(piece(k), k) for k in range(quad - 1, 0, -1)]:
        total = total + got
    other = flip_z(jnp.where(high == 0, total[1], total[0]), quad)
    total = jnp.where(high == 0, total[0], total[1]) + other
    count = lax.axis_size("dom") // ZS
    for got in [shift_y(total, k) for k in range(1, count)]:
        total = total + got
    other = flip_z(total, quad)
    total = jnp.where(high == 0, jnp.stack([total, other]), jnp.stack([other, total]))
    out = jnp.zeros_like(pieces)
    out = lax.dynamic_update_slice_in_dim(out, total[:, None], low, 1)
    for k in range(quad - 1, 0, -1):
        out = lax.dynamic_update_slice_in_dim(out, flip_z(total, k)[:, None], low ^ k, 1)
    return out.reshape(rows, columns)


def gradient_of(overlap, blocks, images, own_image, prev, cells_total):
    own, cells = prev.shape
    total = overlap.shape[1]
    count = len(blocks)
    devices = lax.axis_size("orb") * lax.axis_size("dom")
    chunk = 1024

    def kernel(s_ref, p_ref, *rest):
        g_ref, sums_ref, w_ref, acc_ref, hi_ref, lo_ref = rest[-6:]
        own_refs, refs = rest[:2], rest[2 : 2 + 2 * count]

        @pl.when(pl.program_id(0) == 0)
        def _():
            for index in range(2):
                hi, lo = split(s_ref[(1 - index) * own : (2 - index) * own, :] * (-2.0 / cells_total))
                w_ref[:own, index * total : (index + 1) * total] = hi
                w_ref[own:, index * total : (index + 1) * total] = lo
            acc_ref[...] = jnp.zeros_like(acc_ref)

        store_split(refs, hi_ref, lo_ref)
        with_hi = jnp.dot(w_ref[...], hi_ref[...], preferred_element_type=jnp.float32)
        grad = with_hi[:own] + with_hi[own:]
        grad = grad + jnp.dot(w_ref[:own, :], lo_ref[...], preferred_element_type=jnp.float32)
        grad = grad + 4.0 * jnp.concatenate([own_refs[0][...], own_refs[1][...]], axis=0)
        g_ref[...] = grad
        prev_block = p_ref[...]

        def folded(v):
            v = v.reshape(own // 8, 8, chunk).sum(0)
            return sum(v[:, k * 128 : (k + 1) * 128] for k in range(chunk // 128))

        acc_ref[0:8, :] += folded(grad * grad)
        acc_ref[8:16, :] += folded(grad * prev_block)
        acc_ref[16:24, :] += folded(prev_block * prev_block)

        @pl.when(pl.program_id(0) == cells // chunk - 1)
        def _():
            lane = lax.broadcasted_iota(jnp.int32, (devices, 128), 1)
            row = jnp.zeros((devices, 128), jnp.float32)
            for k in range(3):
                value = acc_ref[8 * k : 8 * k + 8, :].sum(axis=0, keepdims=True).sum(axis=1, keepdims=True)
                row = jnp.where(lane == k, value, row)
            sums_ref[...] = row

    own_block = pl.BlockSpec((own, chunk), lambda i: (0, i))
    column = [pl.BlockSpec((b.shape[0], chunk), lambda i: (0, i)) for b in own_image + blocks + images]
    return pl.pallas_call(
        kernel,
        out_shape=(
            jax.ShapeDtypeStruct((own, cells), jnp.float32),
            jax.ShapeDtypeStruct((devices, 128), jnp.float32),
        ),
        grid=(cells // chunk,),
        in_specs=[pl.BlockSpec((2 * own, total), lambda i: (0, 0)), own_block] + column,
        out_specs=(own_block, pl.BlockSpec((devices, 128), lambda i: (0, 0))),
        scratch_shapes=[
            pltpu.VMEM((2 * own, 2 * total), jnp.bfloat16),
            pltpu.VMEM((24, 128), jnp.float32),
            pltpu.VMEM((2 * total, chunk), jnp.bfloat16),
            pltpu.VMEM((2 * total, chunk), jnp.bfloat16),
        ],
        compiler_params=pltpu.CompilerParams(vmem_limit_bytes=VMEM_LIMIT),
        cost_estimate=pl.CostEstimate(
            flops=12 * own * total * cells, bytes_accessed=8 * cells * total, transcendentals=0
        ),
        name="gradient",
    )(overlap, prev, *own_image, *blocks, *images)


def advance(sums, orbitals, prev_direction, grad):
    step = 16
    rows = orbitals.shape[0]

    def kernel(s_ref, c_ref, d_ref, g_ref, new_ref, dir_ref):
        total = s_ref[...].sum(axis=0, keepdims=True)
        beta = (total[:, 0:1] - total[:, 1:2]) / total[:, 2:3]
        direction = beta[:, None, None, :] * d_ref[...] - g_ref[...]
        dir_ref[...] = direction
        new_ref[...] = c_ref[...] + step_length * direction

    block = pl.BlockSpec((step,) + orbitals.shape[1:], lambda i: (i, 0, 0, 0))
    out = jax.ShapeDtypeStruct(orbitals.shape, jnp.float32)
    return pl.pallas_call(
        kernel,
        out_shape=(out, out),
        grid=(rows // step,),
        in_specs=[pl.BlockSpec(sums.shape, lambda i: (0, 0)), block, block, block],
        out_specs=(block, block),
        cost_estimate=pl.CostEstimate(flops=4 * orbitals.size, bytes_accessed=20 * orbitals.size, transcendentals=0),
        name="advance",
    )(sums, orbitals, prev_direction, grad)


def on_device(orbitals, potential, prev_gradient, prev_direction):
    own = orbitals.shape[0]
    half = own // 2
    slabs = lax.axis_size("dom")
    c = [orbitals[:half].reshape(half, -1), orbitals[half:].reshape(half, -1)]
    near = gather_near(*c)
    far = gather_far(near)
    image = []
    for index in range(2):
        left = lax.ppermute(c[index], "dom", [(i, i + 1) for i in range(slabs - 1)])
        right = lax.ppermute(c[index], "dom", [(i + 1, i) for i in range(slabs - 1)])
        if index == 0:
            prev, left = lax.optimization_barrier((prev_gradient.reshape(own, -1), left))
        image.append(apply_hamiltonian(c[index], left, right, potential.reshape(1, -1)))
    near_image = gather_near(*image)
    far_image = gather_far(near_image)
    part_near = gram(c + image, near)
    part_far = gram(c + image, far)
    overlap = sum_over_slabs(jnp.concatenate([part_near, part_far], axis=1))
    grad, sums = gradient_of(
        overlap, near + far, near_image + far_image, image, prev, slabs * c[0].shape[1]
    )
    sums = lax.all_to_all(sums, ("orb", "dom"), split_axis=0, concat_axis=0, tiled=True)
    grad = grad.reshape(orbitals.shape)
    return (*advance(sums, orbitals, prev_direction, grad), grad)


def solution(mesh):
    in_specs = (
        P("orb", "dom", None, None),
        P("dom", None, None),
        P("orb", "dom", None, None),
        P("orb", "dom", None, None),
    )
    out_specs = (
        P("orb", "dom", None, None),
        P("orb", "dom", None, None),
        P("orb", "dom", None, None),
    )
    return jax.shard_map(
        on_device, mesh=mesh, in_specs=in_specs, out_specs=out_specs, check_vma=False
    )
```

```python
import jax
import jax.numpy as jnp
from jax import lax
from jax.experimental import pallas as pl
from jax.experimental.pallas import tpu as pltpu
from jax.sharding import PartitionSpec as P

coeffs = (-205.0 / 72.0, 8.0 / 5.0, -1.0 / 5.0, 8.0 / 315.0, -1.0 / 560.0)
step_length = 0.05
VMEM_LIMIT = 32 * 1024 * 1024
ZS = 8


def shift_orb(v, k):
    n = lax.axis_size("orb")
    return lax.ppermute(v, "orb", [(i, (i + k) % n) for i in range(n)])


def swap_core(v):
    n = lax.axis_size("orb")
    return lax.ppermute(v, "orb", [(i, i ^ 1) for i in range(n)])


def flip_z(v):
    n = lax.axis_size("dom")
    return lax.ppermute(v, "dom", [(i, i ^ 1) for i in range(n)])


def shift_z(v, k):
    n = lax.axis_size("dom")
    return lax.ppermute(v, "dom", [(i, (i // ZS) * ZS + (i + k) % ZS) for i in range(n)])


def shift_y(v, k):
    n = lax.axis_size("dom")
    return lax.ppermute(v, "dom", [(i, (i + k * ZS) % n) for i in range(n)])


def gather_near(first, second):
    right1, left2 = shift_orb(first, 2), shift_orb(second, -2)
    right2, left1 = shift_orb(second, 2), shift_orb(first, -2)
    blocks = [first, second, right1, left2, right2, left1]
    return blocks + [swap_core(b) for b in blocks]


def gather_far(near):
    far1, far2 = shift_orb(near[2], 2), shift_orb(near[3], -2)
    return [far1, far2, swap_core(far1), swap_core(far2)]


def stencil_kernel(c_ref, l_ref, r_ref, v_ref, o_ref):
    lane = lax.broadcasted_iota(jnp.int32, (8, 128), 1)

    @pl.loop(0, c_ref.shape[0] // 8)
    def _(group):
        rows = pl.ds(pl.multiple_of(group * 8, 8), 8)

        def tile(ref, plane, line):
            start = (plane * 8 + line) * 128
            return ref[rows, start : start + 128]

        def plane_tile(plane, line):
            if plane < 0:
                return tile(l_ref, plane + 4, line)
            if plane > 3:
                return tile(r_ref, plane - 4, line)
            return tile(c_ref, plane, line)

        for plane in range(4):
            for line in range(8):
                start = (plane * 8 + line) * 128
                center = tile(c_ref, plane, line)
                total = (v_ref[:, start : start + 128] - 1.5 * coeffs[0]) * center
                for k in range(1, 5):
                    near = plane_tile(plane + k, line) + plane_tile(plane - k, line)
                    if line + k < 8:
                        near = near + tile(c_ref, plane, line + k)
                    if line - k >= 0:
                        near = near + tile(c_ref, plane, line - k)
                    near = near + jnp.where(lane < 128 - k, pltpu.roll(center, 128 - k, 1), 0.0)
                    near = near + jnp.where(lane >= k, pltpu.roll(center, k, 1), 0.0)
                    total = total + (-0.5 * coeffs[k]) * near
                o_ref[rows, start : start + 128] = total


def apply_hamiltonian(c, left, right, pot):
    rows, cells = c.shape
    step = 24
    block = pl.BlockSpec((step, cells), lambda i: (i, 0))
    return pl.pallas_call(
        stencil_kernel,
        out_shape=jax.ShapeDtypeStruct(c.shape, jnp.float32),
        grid=(rows // step,),
        in_specs=[block, block, block, pl.BlockSpec((1, cells), lambda i: (0, 0))],
        out_specs=block,
        cost_estimate=pl.CostEstimate(flops=40 * rows * cells, bytes_accessed=16 * rows * cells, transcendentals=0),
        name="hamiltonian",
    )(c, left, right, pot)


def split(v):
    hi = v.astype(jnp.bfloat16)
    return hi, (v - hi.astype(jnp.float32)).astype(jnp.bfloat16)


def dot_nt(a, b):
    return lax.dot_general(a, b, (((1,), (1,)), ((), ())), preferred_element_type=jnp.float32)


def store_split(refs, hi_ref, lo_ref):
    at = 0
    for ref in refs:
        hi, lo = split(ref[...])
        hi_ref[at : at + ref.shape[0], :] = hi
        lo_ref[at : at + ref.shape[0], :] = lo
        at += ref.shape[0]


def gram(own_blocks, blocks):
    cells = blocks[0].shape[1]
    count = len(own_blocks)
    rows = sum(b.shape[0] for b in own_blocks)
    total = sum(b.shape[0] for b in blocks)
    chunk = 1024

    def kernel(*rest):
        o_ref, hi_ref, lo_ref, w_ref = rest[-4:]
        store_split(rest[count:-4], hi_ref, lo_ref)
        store_split(rest[:count], w_ref.at[0:rows], w_ref.at[rows : 2 * rows])
        with_hi = dot_nt(w_ref[...], hi_ref[...])
        part = with_hi[:rows] + with_hi[rows:] + dot_nt(w_ref[0:rows, :], lo_ref[...])

        @pl.when(pl.program_id(0) == 0)
        def _():
            o_ref[...] = part

        @pl.when(pl.program_id(0) > 0)
        def _():
            o_ref[...] += part

    return pl.pallas_call(
        kernel,
        out_shape=jax.ShapeDtypeStruct((rows, total), jnp.float32),
        grid=(cells // chunk,),
        in_specs=[pl.BlockSpec((b.shape[0], chunk), lambda i: (0, i)) for b in own_blocks + blocks],
        out_specs=pl.BlockSpec((rows, total), lambda i: (0, 0)),
        scratch_shapes=[
            pltpu.VMEM((total, chunk), jnp.bfloat16),
            pltpu.VMEM((total, chunk), jnp.bfloat16),
            pltpu.VMEM((2 * rows, chunk), jnp.bfloat16),
        ],
        compiler_params=pltpu.CompilerParams(vmem_limit_bytes=VMEM_LIMIT),
        cost_estimate=pl.CostEstimate(
            flops=6 * rows * total * cells, bytes_accessed=4 * cells * (rows + total), transcendentals=0
        ),
        name="gram",
    )(*own_blocks, *blocks)


def sum_over_slabs(part):
    rows, columns = part.shape
    quad = ZS // 2
    z = lax.rem(lax.axis_index("dom"), ZS)
    even = lax.rem(z, 2) == 0
    slot = z // 2
    pieces = part.reshape(quad, 2, rows // ZS, columns)
    order = sorted(range(1, quad), key=lambda k: -min(k, quad - k))

    def piece(k):
        return lax.dynamic_index_in_dim(pieces, lax.rem(slot + k, quad), 0, keepdims=False)

    total = piece(0)
    for got in [shift_z(piece(k), 2 * k) for k in order]:
        total = total + got
    other = flip_z(jnp.where(even, total[1], total[0]))
    total = jnp.where(even, total[0], total[1]) + other
    count = lax.axis_size("dom") // ZS
    for got in [shift_y(total, k) for k in range(1, count)]:
        total = total + got
    other = flip_z(total)
    total = jnp.where(even, jnp.stack([total, other]), jnp.stack([other, total]))
    out = jnp.zeros_like(pieces)
    out = lax.dynamic_update_slice_in_dim(out, total[None], slot, 0)
    for k in order:
        out = lax.dynamic_update_slice_in_dim(out, shift_z(total, 2 * k)[None], lax.rem(slot - k + quad, quad), 0)
    return out.reshape(rows, columns)


def gradient_of(overlap, blocks, images, own_image, prev, cells_total):
    own, cells = prev.shape
    total = overlap.shape[1]
    count = len(blocks)
    devices = lax.axis_size("orb") * lax.axis_size("dom")
    chunk = 1024

    def kernel(s_ref, p_ref, *rest):
        g_ref, sums_ref, w_ref, acc_ref, hi_ref, lo_ref = rest[-6:]
        own_refs, refs = rest[:2], rest[2 : 2 + 2 * count]

        @pl.when(pl.program_id(0) == 0)
        def _():
            for index in range(2):
                hi, lo = split(s_ref[(1 - index) * own : (2 - index) * own, :] * (-2.0 / cells_total))
                w_ref[:own, index * total : (index + 1) * total] = hi
                w_ref[own:, index * total : (index + 1) * total] = lo
            acc_ref[...] = jnp.zeros_like(acc_ref)

        store_split(refs, hi_ref, lo_ref)
        with_hi = jnp.dot(w_ref[...], hi_ref[...], preferred_element_type=jnp.float32)
        grad = with_hi[:own] + with_hi[own:]
        grad = grad + jnp.dot(w_ref[:own, :], lo_ref[...], preferred_element_type=jnp.float32)
        grad = grad + 4.0 * jnp.concatenate([own_refs[0][...], own_refs[1][...]], axis=0)
        g_ref[...] = grad
        prev_block = p_ref[...]

        def folded(v):
            v = v.reshape(own // 8, 8, chunk).sum(0)
            return sum(v[:, k * 128 : (k + 1) * 128] for k in range(chunk // 128))

        acc_ref[0:8, :] += folded(grad * grad)
        acc_ref[8:16, :] += folded(grad * prev_block)
        acc_ref[16:24, :] += folded(prev_block * prev_block)

        @pl.when(pl.program_id(0) == cells // chunk - 1)
        def _():
            lane = lax.broadcasted_iota(jnp.int32, (devices, 128), 1)
            row = jnp.zeros((devices, 128), jnp.float32)
            for k in range(3):
                value = acc_ref[8 * k : 8 * k + 8, :].sum(axis=0, keepdims=True).sum(axis=1, keepdims=True)
                row = jnp.where(lane == k, value, row)
            sums_ref[...] = row

    own_block = pl.BlockSpec((own, chunk), lambda i: (0, i))
    column = [pl.BlockSpec((b.shape[0], chunk), lambda i: (0, i)) for b in own_image + blocks + images]
    return pl.pallas_call(
        kernel,
        out_shape=(
            jax.ShapeDtypeStruct((own, cells), jnp.float32),
            jax.ShapeDtypeStruct((devices, 128), jnp.float32),
        ),
        grid=(cells // chunk,),
        in_specs=[pl.BlockSpec((2 * own, total), lambda i: (0, 0)), own_block] + column,
        out_specs=(own_block, pl.BlockSpec((devices, 128), lambda i: (0, 0))),
        scratch_shapes=[
            pltpu.VMEM((2 * own, 2 * total), jnp.bfloat16),
            pltpu.VMEM((24, 128), jnp.float32),
            pltpu.VMEM((2 * total, chunk), jnp.bfloat16),
            pltpu.VMEM((2 * total, chunk), jnp.bfloat16),
        ],
        compiler_params=pltpu.CompilerParams(vmem_limit_bytes=VMEM_LIMIT),
        cost_estimate=pl.CostEstimate(
            flops=12 * own * total * cells, bytes_accessed=8 * cells * total, transcendentals=0
        ),
        name="gradient",
    )(overlap, prev, *own_image, *blocks, *images)


def advance(sums, orbitals, prev_direction, grad):
    step = 48
    rows = orbitals.shape[0]

    def kernel(s_ref, c_ref, d_ref, g_ref, new_ref, dir_ref):
        total = s_ref[...].sum(axis=0, keepdims=True)
        beta = (total[:, 0:1] - total[:, 1:2]) / total[:, 2:3]
        direction = beta[:, None, None, :] * d_ref[...] - g_ref[...]
        dir_ref[...] = direction
        new_ref[...] = c_ref[...] + step_length * direction

    block = pl.BlockSpec((step,) + orbitals.shape[1:], lambda i: (i, 0, 0, 0))
    out = jax.ShapeDtypeStruct(orbitals.shape, jnp.float32)
    return pl.pallas_call(
        kernel,
        out_shape=(out, out),
        grid=(rows // step,),
        in_specs=[pl.BlockSpec(sums.shape, lambda i: (0, 0)), block, block, block],
        out_specs=(block, block),
        cost_estimate=pl.CostEstimate(flops=4 * orbitals.size, bytes_accessed=20 * orbitals.size, transcendentals=0),
        name="advance",
    )(sums, orbitals, prev_direction, grad)


def on_device(orbitals, potential, prev_gradient, prev_direction):
    own = orbitals.shape[0]
    half = own // 2
    slabs = lax.axis_size("dom")
    c = [orbitals[:half].reshape(half, -1), orbitals[half:].reshape(half, -1)]
    near = gather_near(*c)
    far = gather_far(near)
    image = []
    for index in range(2):
        left = lax.ppermute(c[index], "dom", [(i, i + 1) for i in range(slabs - 1)])
        right = lax.ppermute(c[index], "dom", [(i + 1, i) for i in range(slabs - 1)])
        if index == 0:
            prev, left = lax.optimization_barrier((prev_gradient.reshape(own, -1), left))
        image.append(apply_hamiltonian(c[index], left, right, potential.reshape(1, -1)))
    near_image = gather_near(*image)
    far_image = gather_far(near_image)
    part_near = gram(c + image, near)
    part_far = gram(c + image, far)
    overlap = sum_over_slabs(jnp.concatenate([part_near, part_far], axis=1))
    grad, sums = gradient_of(
        overlap, near + far, near_image + far_image, image, prev, slabs * c[0].shape[1]
    )
    sums = lax.all_to_all(sums, ("orb", "dom"), split_axis=0, concat_axis=0, tiled=True)
    grad = grad.reshape(orbitals.shape)
    return (*advance(sums, orbitals, prev_direction, grad), grad)


def solution(mesh):
    in_specs = (
        P("orb", "dom", None, None),
        P("dom", None, None),
        P("orb", "dom", None, None),
        P("orb", "dom", None, None),
    )
    out_specs = (
        P("orb", "dom", None, None),
        P("orb", "dom", None, None),
        P("orb", "dom", None, None),
    )
    return jax.shard_map(
        on_device, mesh=mesh, in_specs=in_specs, out_specs=out_specs, check_vma=False
    )
```

```python
import jax
import jax.numpy as jnp
from jax import lax
from jax.experimental import pallas as pl
from jax.experimental.pallas import tpu as pltpu
from jax.sharding import PartitionSpec as P

coeffs = (-205.0 / 72.0, 8.0 / 5.0, -1.0 / 5.0, 8.0 / 315.0, -1.0 / 560.0)
step_length = 0.05
VMEM_LIMIT = 56 * 1024 * 1024
ZS = 8


def shift_orb(v, k):
    n = lax.axis_size("orb")
    return lax.ppermute(v, "orb", [(i, (i + k) % n) for i in range(n)])


def swap_core(v):
    n = lax.axis_size("orb")
    return lax.ppermute(v, "orb", [(i, i ^ 1) for i in range(n)])


def flip_z(v):
    n = lax.axis_size("dom")
    return lax.ppermute(v, "dom", [(i, i ^ 1) for i in range(n)])


def shift_z(v, k):
    n = lax.axis_size("dom")
    return lax.ppermute(v, "dom", [(i, (i // ZS) * ZS + (i + k) % ZS) for i in range(n)])


def shift_y(v, k):
    n = lax.axis_size("dom")
    return lax.ppermute(v, "dom", [(i, (i + k * ZS) % n) for i in range(n)])


def gather_near(first, second):
    right1, left2 = shift_orb(first, 2), shift_orb(second, -2)
    right2, left1 = shift_orb(second, 2), shift_orb(first, -2)
    blocks = [first, second, right1, left2, right2, left1]
    return blocks + [swap_core(b) for b in blocks]


def gather_far(near):
    far1, far2 = shift_orb(near[2], 2), shift_orb(near[3], -2)
    return [far1, far2, swap_core(far1), swap_core(far2)]


def stencil_kernel(c_ref, l_ref, r_ref, v_ref, o_ref):
    lane = lax.broadcasted_iota(jnp.int32, (8, 128), 1)

    @pl.loop(0, c_ref.shape[0] // 8)
    def _(group):
        rows = pl.ds(pl.multiple_of(group * 8, 8), 8)

        def tile(ref, plane, line):
            start = (plane * 8 + line) * 128
            return ref[rows, start : start + 128]

        def plane_tile(plane, line):
            if plane < 0:
                return tile(l_ref, plane + 4, line)
            if plane > 3:
                return tile(r_ref, plane - 4, line)
            return tile(c_ref, plane, line)

        for plane in range(4):
            for line in range(8):
                start = (plane * 8 + line) * 128
                center = tile(c_ref, plane, line)
                total = (v_ref[:, start : start + 128] - 1.5 * coeffs[0]) * center
                for k in range(1, 5):
                    near = plane_tile(plane + k, line) + plane_tile(plane - k, line)
                    if line + k < 8:
                        near = near + tile(c_ref, plane, line + k)
                    if line - k >= 0:
                        near = near + tile(c_ref, plane, line - k)
                    near = near + jnp.where(lane < 128 - k, pltpu.roll(center, 128 - k, 1), 0.0)
                    near = near + jnp.where(lane >= k, pltpu.roll(center, k, 1), 0.0)
                    total = total + (-0.5 * coeffs[k]) * near
                o_ref[rows, start : start + 128] = total


def apply_hamiltonian(c, left, right, pot):
    rows, cells = c.shape
    step = 24
    block = pl.BlockSpec((step, cells), lambda i: (i, 0))
    return pl.pallas_call(
        stencil_kernel,
        out_shape=jax.ShapeDtypeStruct(c.shape, jnp.float32),
        grid=(rows // step,),
        in_specs=[block, block, block, pl.BlockSpec((1, cells), lambda i: (0, 0))],
        out_specs=block,
        cost_estimate=pl.CostEstimate(flops=40 * rows * cells, bytes_accessed=16 * rows * cells, transcendentals=0),
        name="hamiltonian",
    )(c, left, right, pot)


def split(v):
    hi = v.astype(jnp.bfloat16)
    return hi, (v - hi.astype(jnp.float32)).astype(jnp.bfloat16)


def dot_nt(a, b):
    return lax.dot_general(a, b, (((1,), (1,)), ((), ())), preferred_element_type=jnp.float32)


def store_split(refs, hi_ref, lo_ref):
    at = 0
    for ref in refs:
        hi, lo = split(ref[...])
        hi_ref[at : at + ref.shape[0], :] = hi
        lo_ref[at : at + ref.shape[0], :] = lo
        at += ref.shape[0]


def gram(own_blocks, blocks):
    cells = blocks[0].shape[1]
    count = len(own_blocks)
    rows = sum(b.shape[0] for b in own_blocks)
    total = sum(b.shape[0] for b in blocks)
    chunk = 1024

    def kernel(*rest):
        o_ref, hi_ref, lo_ref, w_ref = rest[-4:]
        store_split(rest[count:-4], hi_ref, lo_ref)
        store_split(rest[:count], w_ref.at[0:rows], w_ref.at[rows : 2 * rows])
        with_hi = dot_nt(w_ref[...], hi_ref[...])
        part = with_hi[:rows] + with_hi[rows:] + dot_nt(w_ref[0:rows, :], lo_ref[...])

        @pl.when(pl.program_id(0) == 0)
        def _():
            o_ref[...] = part

        @pl.when(pl.program_id(0) > 0)
        def _():
            o_ref[...] += part

    return pl.pallas_call(
        kernel,
        out_shape=jax.ShapeDtypeStruct((rows, total), jnp.float32),
        grid=(cells // chunk,),
        in_specs=[pl.BlockSpec((b.shape[0], chunk), lambda i: (0, i)) for b in own_blocks + blocks],
        out_specs=pl.BlockSpec((rows, total), lambda i: (0, 0)),
        scratch_shapes=[
            pltpu.VMEM((total, chunk), jnp.bfloat16),
            pltpu.VMEM((total, chunk), jnp.bfloat16),
            pltpu.VMEM((2 * rows, chunk), jnp.bfloat16),
        ],
        compiler_params=pltpu.CompilerParams(vmem_limit_bytes=VMEM_LIMIT),
        cost_estimate=pl.CostEstimate(
            flops=6 * rows * total * cells, bytes_accessed=4 * cells * (rows + total), transcendentals=0
        ),
        name="gram",
    )(*own_blocks, *blocks)


def sum_over_slabs(part):
    rows, columns = part.shape
    slabs = lax.axis_size("dom")
    count = slabs // ZS
    dom = lax.axis_index("dom")
    slot = dom // ZS
    even = lax.rem(dom, 2) == 0
    pieces = part.reshape(count, 2, rows // (2 * count), columns)
    quad = ZS // 2

    def piece(k):
        return lax.dynamic_index_in_dim(pieces, lax.rem(slot + k, count), 0, keepdims=False)

    total = piece(0)
    order = sorted(range(1, count), key=lambda k: -min(k, count - k))
    for got in [shift_y(piece(k), k) for k in order]:
        total = total + got
    other = flip_z(jnp.where(even, total[1], total[0]))
    total = jnp.where(even, total[0], total[1]) + other
    for got in [shift_z(total, 2 * k) for k in sorted(range(1, quad), key=lambda k: -min(k, quad - k))]:
        total = total + got
    other = flip_z(total)
    total = jnp.where(even, jnp.stack([total, other]), jnp.stack([other, total]))
    out = jnp.zeros_like(pieces)
    out = lax.dynamic_update_slice_in_dim(out, total[None], slot, 0)
    for k in order:
        out = lax.dynamic_update_slice_in_dim(
            out, shift_y(total, k)[None], lax.rem(slot - k + count, count), 0
        )
    return out.reshape(rows, columns)


def gradient_of(overlap, blocks, images, own_image, prev, cells_total):
    own, cells = prev.shape
    total = overlap.shape[1]
    count = len(blocks)
    devices = lax.axis_size("orb") * lax.axis_size("dom")
    chunk = 1024

    def kernel(s_ref, p_ref, *rest):
        g_ref, sums_ref, w_ref, acc_ref, hi_ref, lo_ref = rest[-6:]
        own_refs, refs = rest[:2], rest[2 : 2 + 2 * count]

        @pl.when(pl.program_id(0) == 0)
        def _():
            for index in range(2):
                hi, lo = split(s_ref[(1 - index) * own : (2 - index) * own, :] * (-2.0 / cells_total))
                w_ref[:own, index * total : (index + 1) * total] = hi
                w_ref[own:, index * total : (index + 1) * total] = lo
            acc_ref[...] = jnp.zeros_like(acc_ref)

        store_split(refs, hi_ref, lo_ref)
        with_hi = jnp.dot(w_ref[...], hi_ref[...], preferred_element_type=jnp.float32)
        grad = with_hi[:own] + with_hi[own:]
        grad = grad + jnp.dot(w_ref[:own, :], lo_ref[...], preferred_element_type=jnp.float32)
        grad = grad + 4.0 * jnp.concatenate([own_refs[0][...], own_refs[1][...]], axis=0)
        g_ref[...] = grad
        prev_block = p_ref[...]

        def folded(v):
            v = v.reshape(own // 8, 8, chunk).sum(0)
            return sum(v[:, k * 128 : (k + 1) * 128] for k in range(chunk // 128))

        acc_ref[0:8, :] += folded(grad * grad)
        acc_ref[8:16, :] += folded(grad * prev_block)
        acc_ref[16:24, :] += folded(prev_block * prev_block)

        @pl.when(pl.program_id(0) == cells // chunk - 1)
        def _():
            lane = lax.broadcasted_iota(jnp.int32, (devices, 128), 1)
            row = jnp.zeros((devices, 128), jnp.float32)
            for k in range(3):
                value = acc_ref[8 * k : 8 * k + 8, :].sum(axis=0, keepdims=True).sum(axis=1, keepdims=True)
                row = jnp.where(lane == k, value, row)
            sums_ref[...] = row

    own_block = pl.BlockSpec((own, chunk), lambda i: (0, i))
    column = [pl.BlockSpec((b.shape[0], chunk), lambda i: (0, i)) for b in own_image + blocks + images]
    return pl.pallas_call(
        kernel,
        out_shape=(
            jax.ShapeDtypeStruct((own, cells), jnp.float32),
            jax.ShapeDtypeStruct((devices, 128), jnp.float32),
        ),
        grid=(cells // chunk,),
        in_specs=[pl.BlockSpec((2 * own, total), lambda i: (0, 0)), own_block] + column,
        out_specs=(own_block, pl.BlockSpec((devices, 128), lambda i: (0, 0))),
        scratch_shapes=[
            pltpu.VMEM((2 * own, 2 * total), jnp.bfloat16),
            pltpu.VMEM((24, 128), jnp.float32),
            pltpu.VMEM((2 * total, chunk), jnp.bfloat16),
            pltpu.VMEM((2 * total, chunk), jnp.bfloat16),
        ],
        compiler_params=pltpu.CompilerParams(vmem_limit_bytes=VMEM_LIMIT),
        cost_estimate=pl.CostEstimate(
            flops=12 * own * total * cells, bytes_accessed=8 * cells * total, transcendentals=0
        ),
        name="gradient",
    )(overlap, prev, *own_image, *blocks, *images)


def advance(sums, orbitals, prev_direction, grad):
    step = 48
    rows = orbitals.shape[0]

    def kernel(s_ref, c_ref, d_ref, g_ref, new_ref, dir_ref):
        total = s_ref[...].sum(axis=0, keepdims=True)
        beta = (total[:, 0:1] - total[:, 1:2]) / total[:, 2:3]
        direction = beta[:, None, None, :] * d_ref[...] - g_ref[...]
        dir_ref[...] = direction
        new_ref[...] = c_ref[...] + step_length * direction

    block = pl.BlockSpec((step,) + orbitals.shape[1:], lambda i: (i, 0, 0, 0))
    out = jax.ShapeDtypeStruct(orbitals.shape, jnp.float32)
    return pl.pallas_call(
        kernel,
        out_shape=(out, out),
        grid=(rows // step,),
        in_specs=[pl.BlockSpec(sums.shape, lambda i: (0, 0)), block, block, block],
        out_specs=(block, block),
        cost_estimate=pl.CostEstimate(flops=4 * orbitals.size, bytes_accessed=20 * orbitals.size, transcendentals=0),
        name="advance",
    )(sums, orbitals, prev_direction, grad)


def on_device(orbitals, potential, prev_gradient, prev_direction):
    own = orbitals.shape[0]
    half = own // 2
    slabs = lax.axis_size("dom")
    c = [orbitals[:half].reshape(half, -1), orbitals[half:].reshape(half, -1)]
    near = gather_near(*c)
    far = gather_far(near)
    image = []
    for index in range(2):
        left = lax.ppermute(c[index], "dom", [(i, i + 1) for i in range(slabs - 1)])
        right = lax.ppermute(c[index], "dom", [(i + 1, i) for i in range(slabs - 1)])
        if index == 0:
            prev, left = lax.optimization_barrier((prev_gradient.reshape(own, -1), left))
        image.append(apply_hamiltonian(c[index], left, right, potential.reshape(1, -1)))
    near_image = gather_near(*image)
    far_image = gather_far(near_image)
    part_near = gram(c + image, near)
    part_far = gram(c + image, far)
    overlap = sum_over_slabs(jnp.concatenate([part_near, part_far], axis=1))
    grad, sums = gradient_of(
        overlap, near + far, near_image + far_image, image, prev, slabs * c[0].shape[1]
    )
    sums = lax.all_to_all(sums, ("orb", "dom"), split_axis=0, concat_axis=0, tiled=True)
    grad = grad.reshape(orbitals.shape)
    return (*advance(sums, orbitals, prev_direction, grad), grad)


def solution(mesh):
    in_specs = (
        P("orb", "dom", None, None),
        P("dom", None, None),
        P("orb", "dom", None, None),
        P("orb", "dom", None, None),
    )
    out_specs = (
        P("orb", "dom", None, None),
        P("orb", "dom", None, None),
        P("orb", "dom", None, None),
    )
    return jax.shard_map(
        on_device, mesh=mesh, in_specs=in_specs, out_specs=out_specs, check_vma=False
    )
```

```python
import jax
import jax.numpy as jnp
from jax import lax
from jax.experimental import pallas as pl
from jax.experimental.pallas import tpu as pltpu
from jax.sharding import PartitionSpec as P

coeffs = (-205.0 / 72.0, 8.0 / 5.0, -1.0 / 5.0, 8.0 / 315.0, -1.0 / 560.0)
step_length = 0.05
GRAM_VMEM = 56 * 1024 * 1024
FAR_VMEM = 24 * 1024 * 1024
GRADIENT_VMEM = 32 * 1024 * 1024
ZS = 8


def shift_orb(v, k):
    n = lax.axis_size("orb")
    return lax.ppermute(v, "orb", [(i, (i + k) % n) for i in range(n)])


def swap_core(v):
    n = lax.axis_size("orb")
    return lax.ppermute(v, "orb", [(i, i ^ 1) for i in range(n)])


def flip_z(v):
    n = lax.axis_size("dom")
    return lax.ppermute(v, "dom", [(i, i ^ 1) for i in range(n)])


def shift_z(v, k):
    n = lax.axis_size("dom")
    return lax.ppermute(v, "dom", [(i, (i // ZS) * ZS + (i + k) % ZS) for i in range(n)])


def shift_y(v, k):
    n = lax.axis_size("dom")
    return lax.ppermute(v, "dom", [(i, (i + k * ZS) % n) for i in range(n)])


def gather_near(first, second):
    right1, left2 = shift_orb(first, 2), shift_orb(second, -2)
    right2, left1 = shift_orb(second, 2), shift_orb(first, -2)
    blocks = [first, second, right1, left2, right2, left1]
    return blocks + [swap_core(b) for b in blocks]


def gather_far(near):
    far1, far2 = shift_orb(near[2], 2), shift_orb(near[3], -2)
    return [far1, far2, swap_core(far1), swap_core(far2)]


def stencil_kernel(c_ref, l_ref, r_ref, v_ref, o_ref):
    lane = lax.broadcasted_iota(jnp.int32, (8, 128), 1)

    @pl.loop(0, c_ref.shape[0] // 8)
    def _(group):
        rows = pl.ds(pl.multiple_of(group * 8, 8), 8)

        def tile(ref, plane, line):
            start = (plane * 8 + line) * 128
            return ref[rows, start : start + 128]

        def plane_tile(plane, line):
            if plane < 0:
                return tile(l_ref, plane + 4, line)
            if plane > 3:
                return tile(r_ref, plane - 4, line)
            return tile(c_ref, plane, line)

        for plane in range(4):
            for line in range(8):
                start = (plane * 8 + line) * 128
                center = tile(c_ref, plane, line)
                total = (v_ref[:, start : start + 128] - 1.5 * coeffs[0]) * center
                for k in range(1, 5):
                    near = plane_tile(plane + k, line) + plane_tile(plane - k, line)
                    if line + k < 8:
                        near = near + tile(c_ref, plane, line + k)
                    if line - k >= 0:
                        near = near + tile(c_ref, plane, line - k)
                    near = near + jnp.where(lane < 128 - k, pltpu.roll(center, 128 - k, 1), 0.0)
                    near = near + jnp.where(lane >= k, pltpu.roll(center, k, 1), 0.0)
                    total = total + (-0.5 * coeffs[k]) * near
                o_ref[rows, start : start + 128] = total


def apply_hamiltonian(c, left, right, pot):
    rows, cells = c.shape
    step = 24
    block = pl.BlockSpec((step, cells), lambda i: (i, 0))
    return pl.pallas_call(
        stencil_kernel,
        out_shape=jax.ShapeDtypeStruct(c.shape, jnp.float32),
        grid=(rows // step,),
        in_specs=[block, block, block, pl.BlockSpec((1, cells), lambda i: (0, 0))],
        out_specs=block,
        cost_estimate=pl.CostEstimate(flops=40 * rows * cells, bytes_accessed=16 * rows * cells, transcendentals=0),
        name="hamiltonian",
    )(c, left, right, pot)


def split(v):
    hi = v.astype(jnp.bfloat16)
    return hi, (v - hi.astype(jnp.float32)).astype(jnp.bfloat16)


def dot_nt(a, b):
    return lax.dot_general(a, b, (((1,), (1,)), ((), ())), preferred_element_type=jnp.float32)


def store_split(refs, hi_ref, lo_ref):
    at = 0
    for ref in refs:
        hi, lo = split(ref[...])
        hi_ref[at : at + ref.shape[0], :] = hi
        lo_ref[at : at + ref.shape[0], :] = lo
        at += ref.shape[0]


def gram(own_blocks, blocks, grant):
    cells = blocks[0].shape[1]
    count = len(own_blocks)
    rows = sum(b.shape[0] for b in own_blocks)
    total = sum(b.shape[0] for b in blocks)
    chunk = 1024

    def kernel(*rest):
        o_ref, hi_ref, lo_ref, w_ref = rest[-4:]
        store_split(rest[count:-4], hi_ref, lo_ref)
        store_split(rest[:count], w_ref.at[0:rows], w_ref.at[rows : 2 * rows])
        with_hi = dot_nt(w_ref[...], hi_ref[...])
        part = with_hi[:rows] + with_hi[rows:] + dot_nt(w_ref[0:rows, :], lo_ref[...])

        @pl.when(pl.program_id(0) == 0)
        def _():
            o_ref[...] = part

        @pl.when(pl.program_id(0) > 0)
        def _():
            o_ref[...] += part

    return pl.pallas_call(
        kernel,
        out_shape=jax.ShapeDtypeStruct((rows, total), jnp.float32),
        grid=(cells // chunk,),
        in_specs=[pl.BlockSpec((b.shape[0], chunk), lambda i: (0, i)) for b in own_blocks + blocks],
        out_specs=pl.BlockSpec((rows, total), lambda i: (0, 0)),
        scratch_shapes=[
            pltpu.VMEM((total, chunk), jnp.bfloat16),
            pltpu.VMEM((total, chunk), jnp.bfloat16),
            pltpu.VMEM((2 * rows, chunk), jnp.bfloat16),
        ],
        compiler_params=pltpu.CompilerParams(vmem_limit_bytes=grant),
        cost_estimate=pl.CostEstimate(
            flops=6 * rows * total * cells, bytes_accessed=4 * cells * (rows + total), transcendentals=0
        ),
        name="gram",
    )(*own_blocks, *blocks)


def sum_over_slabs(part):
    rows, columns = part.shape
    slabs = lax.axis_size("dom")
    count = slabs // ZS
    dom = lax.axis_index("dom")
    slot = dom // ZS
    even = lax.rem(dom, 2) == 0
    pieces = part.reshape(count, 2, rows // (2 * count), columns)
    quad = ZS // 2

    def piece(k):
        return lax.dynamic_index_in_dim(pieces, lax.rem(slot + k, count), 0, keepdims=False)

    total = piece(0)
    order = sorted(range(1, count), key=lambda k: -min(k, count - k))
    for got in [shift_y(piece(k), k) for k in order]:
        total = total + got
    other = flip_z(jnp.where(even, total[1], total[0]))
    total = jnp.where(even, total[0], total[1]) + other
    for got in [shift_z(total, 2 * k) for k in sorted(range(1, quad), key=lambda k: -min(k, quad - k))]:
        total = total + got
    other = flip_z(total)
    total = jnp.where(even, jnp.stack([total, other]), jnp.stack([other, total]))
    out = jnp.zeros_like(pieces)
    out = lax.dynamic_update_slice_in_dim(out, total[None], slot, 0)
    for k in order:
        out = lax.dynamic_update_slice_in_dim(
            out, shift_y(total, k)[None], lax.rem(slot - k + count, count), 0
        )
    return out.reshape(rows, columns)


def gradient_of(overlap, blocks, images, own_image, prev, cells_total):
    own, cells = prev.shape
    total = overlap.shape[1]
    count = len(blocks)
    devices = lax.axis_size("orb") * lax.axis_size("dom")
    chunk = 1024

    def kernel(s_ref, p_ref, *rest):
        g_ref, sums_ref, w_ref, acc_ref, hi_ref, lo_ref = rest[-6:]
        own_refs, refs = rest[:2], rest[2 : 2 + 2 * count]

        @pl.when(pl.program_id(0) == 0)
        def _():
            for index in range(2):
                hi, lo = split(s_ref[(1 - index) * own : (2 - index) * own, :] * (-2.0 / cells_total))
                w_ref[:own, index * total : (index + 1) * total] = hi
                w_ref[own:, index * total : (index + 1) * total] = lo
            acc_ref[...] = jnp.zeros_like(acc_ref)

        store_split(refs, hi_ref, lo_ref)
        with_hi = jnp.dot(w_ref[...], hi_ref[...], preferred_element_type=jnp.float32)
        grad = with_hi[:own] + with_hi[own:]
        grad = grad + jnp.dot(w_ref[:own, :], lo_ref[...], preferred_element_type=jnp.float32)
        grad = grad + 4.0 * jnp.concatenate([own_refs[0][...], own_refs[1][...]], axis=0)
        g_ref[...] = grad
        prev_block = p_ref[...]

        def folded(v):
            v = v.reshape(own // 8, 8, chunk).sum(0)
            return sum(v[:, k * 128 : (k + 1) * 128] for k in range(chunk // 128))

        acc_ref[0:8, :] += folded(grad * grad)
        acc_ref[8:16, :] += folded(grad * prev_block)
        acc_ref[16:24, :] += folded(prev_block * prev_block)

        @pl.when(pl.program_id(0) == cells // chunk - 1)
        def _():
            lane = lax.broadcasted_iota(jnp.int32, (devices, 128), 1)
            row = jnp.zeros((devices, 128), jnp.float32)
            for k in range(3):
                value = acc_ref[8 * k : 8 * k + 8, :].sum(axis=0, keepdims=True).sum(axis=1, keepdims=True)
                row = jnp.where(lane == k, value, row)
            sums_ref[...] = row

    own_block = pl.BlockSpec((own, chunk), lambda i: (0, i))
    column = [pl.BlockSpec((b.shape[0], chunk), lambda i: (0, i)) for b in own_image + blocks + images]
    return pl.pallas_call(
        kernel,
        out_shape=(
            jax.ShapeDtypeStruct((own, cells), jnp.float32),
            jax.ShapeDtypeStruct((devices, 128), jnp.float32),
        ),
        grid=(cells // chunk,),
        in_specs=[pl.BlockSpec((2 * own, total), lambda i: (0, 0)), own_block] + column,
        out_specs=(own_block, pl.BlockSpec((devices, 128), lambda i: (0, 0))),
        scratch_shapes=[
            pltpu.VMEM((2 * own, 2 * total), jnp.bfloat16),
            pltpu.VMEM((24, 128), jnp.float32),
            pltpu.VMEM((2 * total, chunk), jnp.bfloat16),
            pltpu.VMEM((2 * total, chunk), jnp.bfloat16),
        ],
        compiler_params=pltpu.CompilerParams(vmem_limit_bytes=GRADIENT_VMEM),
        cost_estimate=pl.CostEstimate(
            flops=12 * own * total * cells, bytes_accessed=8 * cells * total, transcendentals=0
        ),
        name="gradient",
    )(overlap, prev, *own_image, *blocks, *images)


def advance(sums, orbitals, prev_direction, grad):
    step = 48
    rows = orbitals.shape[0]

    def kernel(s_ref, c_ref, d_ref, g_ref, new_ref, dir_ref):
        total = s_ref[...].sum(axis=0, keepdims=True)
        beta = (total[:, 0:1] - total[:, 1:2]) / total[:, 2:3]
        direction = beta[:, None, None, :] * d_ref[...] - g_ref[...]
        dir_ref[...] = direction
        new_ref[...] = c_ref[...] + step_length * direction

    block = pl.BlockSpec((step,) + orbitals.shape[1:], lambda i: (i, 0, 0, 0))
    out = jax.ShapeDtypeStruct(orbitals.shape, jnp.float32)
    return pl.pallas_call(
        kernel,
        out_shape=(out, out),
        grid=(rows // step,),
        in_specs=[pl.BlockSpec(sums.shape, lambda i: (0, 0)), block, block, block],
        out_specs=(block, block),
        cost_estimate=pl.CostEstimate(flops=4 * orbitals.size, bytes_accessed=20 * orbitals.size, transcendentals=0),
        name="advance",
    )(sums, orbitals, prev_direction, grad)


def on_device(orbitals, potential, prev_gradient, prev_direction):
    own = orbitals.shape[0]
    half = own // 2
    slabs = lax.axis_size("dom")
    c = [orbitals[:half].reshape(half, -1), orbitals[half:].reshape(half, -1)]
    near = gather_near(*c)
    far = gather_far(near)
    image = []
    for index in range(2):
        left = lax.ppermute(c[index], "dom", [(i, i + 1) for i in range(slabs - 1)])
        right = lax.ppermute(c[index], "dom", [(i + 1, i) for i in range(slabs - 1)])
        if index == 0:
            prev, left = lax.optimization_barrier((prev_gradient.reshape(own, -1), left))
        image.append(apply_hamiltonian(c[index], left, right, potential.reshape(1, -1)))
    near_image = gather_near(*image)
    far_image = gather_far(near_image)
    part_a = gram(c + image[:1], near, GRAM_VMEM)
    part_b = gram(image[1:], near, GRAM_VMEM)
    part_far = gram(c + image, far, FAR_VMEM)
    part = jnp.concatenate([jnp.concatenate([part_a, part_b], axis=0), part_far], axis=1)
    overlap = sum_over_slabs(part)
    grad, sums = gradient_of(
        overlap, near + far, near_image + far_image, image, prev, slabs * c[0].shape[1]
    )
    sums = lax.all_to_all(sums, ("orb", "dom"), split_axis=0, concat_axis=0, tiled=True)
    grad = grad.reshape(orbitals.shape)
    return (*advance(sums, orbitals, prev_direction, grad), grad)


def solution(mesh):
    in_specs = (
        P("orb", "dom", None, None),
        P("dom", None, None),
        P("orb", "dom", None, None),
        P("orb", "dom", None, None),
    )
    out_specs = (
        P("orb", "dom", None, None),
        P("orb", "dom", None, None),
        P("orb", "dom", None, None),
    )
    return jax.shard_map(
        on_device, mesh=mesh, in_specs=in_specs, out_specs=out_specs, check_vma=False
    )
```

```python
import jax
import jax.numpy as jnp
from jax import lax
from jax.experimental import pallas as pl
from jax.experimental.pallas import tpu as pltpu
from jax.sharding import PartitionSpec as P

coeffs = (-205.0 / 72.0, 8.0 / 5.0, -1.0 / 5.0, 8.0 / 315.0, -1.0 / 560.0)
step_length = 0.05
GRAM_VMEM = 56 * 1024 * 1024
GRADIENT_VMEM = 32 * 1024 * 1024
ZS = 8


def shift_orb(v, k):
    n = lax.axis_size("orb")
    return lax.ppermute(v, "orb", [(i, (i + k) % n) for i in range(n)])


def swap_core(v):
    n = lax.axis_size("orb")
    return lax.ppermute(v, "orb", [(i, i ^ 1) for i in range(n)])


def flip_z(v):
    n = lax.axis_size("dom")
    return lax.ppermute(v, "dom", [(i, i ^ 1) for i in range(n)])


def shift_z(v, k):
    n = lax.axis_size("dom")
    return lax.ppermute(v, "dom", [(i, (i // ZS) * ZS + (i + k) % ZS) for i in range(n)])


def shift_y(v, k):
    n = lax.axis_size("dom")
    return lax.ppermute(v, "dom", [(i, (i + k * ZS) % n) for i in range(n)])


def gather_near(first, second):
    right1, left2 = shift_orb(first, 2), shift_orb(second, -2)
    right2, left1 = shift_orb(second, 2), shift_orb(first, -2)
    blocks = [first, second, right1, left2, right2, left1]
    return blocks + [swap_core(b) for b in blocks]


def gather_far(near):
    far1, far2 = shift_orb(near[2], 2), shift_orb(near[3], -2)
    return [far1, far2, swap_core(far1), swap_core(far2)]


def stencil_kernel(c_ref, l_ref, r_ref, v_ref, o_ref):
    lane = lax.broadcasted_iota(jnp.int32, (8, 128), 1)

    @pl.loop(0, c_ref.shape[0] // 8)
    def _(group):
        rows = pl.ds(pl.multiple_of(group * 8, 8), 8)

        def tile(ref, plane, line):
            start = (plane * 8 + line) * 128
            return ref[rows, start : start + 128]

        def plane_tile(plane, line):
            if plane < 0:
                return tile(l_ref, plane + 4, line)
            if plane > 3:
                return tile(r_ref, plane - 4, line)
            return tile(c_ref, plane, line)

        for plane in range(4):
            for line in range(8):
                start = (plane * 8 + line) * 128
                center = tile(c_ref, plane, line)
                total = (v_ref[:, start : start + 128] - 1.5 * coeffs[0]) * center
                for k in range(1, 5):
                    near = plane_tile(plane + k, line) + plane_tile(plane - k, line)
                    if line + k < 8:
                        near = near + tile(c_ref, plane, line + k)
                    if line - k >= 0:
                        near = near + tile(c_ref, plane, line - k)
                    near = near + jnp.where(lane < 128 - k, pltpu.roll(center, 128 - k, 1), 0.0)
                    near = near + jnp.where(lane >= k, pltpu.roll(center, k, 1), 0.0)
                    total = total + (-0.5 * coeffs[k]) * near
                o_ref[rows, start : start + 128] = total


def apply_hamiltonian(c, left, right, pot):
    rows, cells = c.shape
    step = 24
    block = pl.BlockSpec((step, cells), lambda i: (i, 0))
    return pl.pallas_call(
        stencil_kernel,
        out_shape=jax.ShapeDtypeStruct(c.shape, jnp.float32),
        grid=(rows // step,),
        in_specs=[block, block, block, pl.BlockSpec((1, cells), lambda i: (0, 0))],
        out_specs=block,
        cost_estimate=pl.CostEstimate(flops=40 * rows * cells, bytes_accessed=16 * rows * cells, transcendentals=0),
        name="hamiltonian",
    )(c, left, right, pot)


def split(v):
    hi = v.astype(jnp.bfloat16)
    return hi, (v - hi.astype(jnp.float32)).astype(jnp.bfloat16)


def dot_nt(a, b):
    return lax.dot_general(a, b, (((1,), (1,)), ((), ())), preferred_element_type=jnp.float32)


def store_split(refs, hi_ref, lo_ref):
    at = 0
    for ref in refs:
        hi, lo = split(ref[...])
        hi_ref[at : at + ref.shape[0], :] = hi
        lo_ref[at : at + ref.shape[0], :] = lo
        at += ref.shape[0]


def gram(own_blocks, blocks):
    cells = blocks[0].shape[1]
    count = len(own_blocks)
    rows = sum(b.shape[0] for b in own_blocks)
    total = sum(b.shape[0] for b in blocks)
    chunk = 1024

    def kernel(*rest):
        o_ref, hi_ref, lo_ref, w_ref = rest[-4:]
        store_split(rest[count:-4], hi_ref, lo_ref)
        store_split(rest[:count], w_ref.at[0:rows], w_ref.at[rows : 2 * rows])
        with_hi = dot_nt(w_ref[...], hi_ref[...])
        part = with_hi[:rows] + with_hi[rows:] + dot_nt(w_ref[0:rows, :], lo_ref[...])

        @pl.when(pl.program_id(0) == 0)
        def _():
            o_ref[...] = part

        @pl.when(pl.program_id(0) > 0)
        def _():
            o_ref[...] += part

    return pl.pallas_call(
        kernel,
        out_shape=jax.ShapeDtypeStruct((rows, total), jnp.float32),
        grid=(cells // chunk,),
        in_specs=[pl.BlockSpec((b.shape[0], chunk), lambda i: (0, i)) for b in own_blocks + blocks],
        out_specs=pl.BlockSpec((rows, total), lambda i: (0, 0)),
        scratch_shapes=[
            pltpu.VMEM((total, chunk), jnp.bfloat16),
            pltpu.VMEM((total, chunk), jnp.bfloat16),
            pltpu.VMEM((2 * rows, chunk), jnp.bfloat16),
        ],
        compiler_params=pltpu.CompilerParams(vmem_limit_bytes=GRAM_VMEM),
        cost_estimate=pl.CostEstimate(
            flops=6 * rows * total * cells, bytes_accessed=4 * cells * (rows + total), transcendentals=0
        ),
        name="gram",
    )(*own_blocks, *blocks)


def sum_over_slabs(part):
    rows, columns = part.shape
    slabs = lax.axis_size("dom")
    count = slabs // ZS
    dom = lax.axis_index("dom")
    slot = dom // ZS
    even = lax.rem(dom, 2) == 0
    pieces = part.reshape(count, 2, rows // (2 * count), columns)
    quad = ZS // 2

    def piece(k):
        return lax.dynamic_index_in_dim(pieces, lax.rem(slot + k, count), 0, keepdims=False)

    total = piece(0)
    order = sorted(range(1, count), key=lambda k: -min(k, count - k))
    for got in [shift_y(piece(k), k) for k in order]:
        total = total + got
    other = flip_z(jnp.where(even, total[1], total[0]))
    total = jnp.where(even, total[0], total[1]) + other
    for got in [shift_z(total, 2 * k) for k in sorted(range(1, quad), key=lambda k: -min(k, quad - k))]:
        total = total + got
    other = flip_z(total)
    total = jnp.where(even, jnp.stack([total, other]), jnp.stack([other, total]))
    out = jnp.zeros_like(pieces)
    out = lax.dynamic_update_slice_in_dim(out, total[None], slot, 0)
    for k in order:
        out = lax.dynamic_update_slice_in_dim(
            out, shift_y(total, k)[None], lax.rem(slot - k + count, count), 0
        )
    return out.reshape(rows, columns)


def gradient_of(overlap, blocks, images, own_image, prev, cells_total):
    own, cells = prev.shape
    total = overlap.shape[1]
    count = len(blocks)
    devices = lax.axis_size("orb") * lax.axis_size("dom")
    chunk = 1024

    def kernel(s_ref, p_ref, *rest):
        g_ref, sums_ref, w_ref, acc_ref, hi_ref, lo_ref = rest[-6:]
        own_refs, refs = rest[:2], rest[2 : 2 + 2 * count]

        @pl.when(pl.program_id(0) == 0)
        def _():
            for index in range(2):
                hi, lo = split(s_ref[(1 - index) * own : (2 - index) * own, :] * (-2.0 / cells_total))
                w_ref[:own, index * total : (index + 1) * total] = hi
                w_ref[own:, index * total : (index + 1) * total] = lo
            acc_ref[...] = jnp.zeros_like(acc_ref)

        store_split(refs, hi_ref, lo_ref)
        with_hi = jnp.dot(w_ref[...], hi_ref[...], preferred_element_type=jnp.float32)
        grad = with_hi[:own] + with_hi[own:]
        grad = grad + jnp.dot(w_ref[:own, :], lo_ref[...], preferred_element_type=jnp.float32)
        grad = grad + 4.0 * jnp.concatenate([own_refs[0][...], own_refs[1][...]], axis=0)
        g_ref[...] = grad
        prev_block = p_ref[...]

        def folded(v):
            v = v.reshape(own // 8, 8, chunk).sum(0)
            return sum(v[:, k * 128 : (k + 1) * 128] for k in range(chunk // 128))

        acc_ref[0:8, :] += folded(grad * grad)
        acc_ref[8:16, :] += folded(grad * prev_block)
        acc_ref[16:24, :] += folded(prev_block * prev_block)

        @pl.when(pl.program_id(0) == cells // chunk - 1)
        def _():
            lane = lax.broadcasted_iota(jnp.int32, (devices, 128), 1)
            row = jnp.zeros((devices, 128), jnp.float32)
            for k in range(3):
                value = acc_ref[8 * k : 8 * k + 8, :].sum(axis=0, keepdims=True).sum(axis=1, keepdims=True)
                row = jnp.where(lane == k, value, row)
            sums_ref[...] = row

    own_block = pl.BlockSpec((own, chunk), lambda i: (0, i))
    column = [pl.BlockSpec((b.shape[0], chunk), lambda i: (0, i)) for b in own_image + blocks + images]
    return pl.pallas_call(
        kernel,
        out_shape=(
            jax.ShapeDtypeStruct((own, cells), jnp.float32),
            jax.ShapeDtypeStruct((devices, 128), jnp.float32),
        ),
        grid=(cells // chunk,),
        in_specs=[pl.BlockSpec((2 * own, total), lambda i: (0, 0)), own_block] + column,
        out_specs=(own_block, pl.BlockSpec((devices, 128), lambda i: (0, 0))),
        scratch_shapes=[
            pltpu.VMEM((2 * own, 2 * total), jnp.bfloat16),
            pltpu.VMEM((24, 128), jnp.float32),
            pltpu.VMEM((2 * total, chunk), jnp.bfloat16),
            pltpu.VMEM((2 * total, chunk), jnp.bfloat16),
        ],
        compiler_params=pltpu.CompilerParams(vmem_limit_bytes=GRADIENT_VMEM),
        cost_estimate=pl.CostEstimate(
            flops=12 * own * total * cells, bytes_accessed=8 * cells * total, transcendentals=0
        ),
        name="gradient",
    )(overlap, prev, *own_image, *blocks, *images)


def advance(sums, orbitals, prev_direction, grad):
    step = 48
    rows = orbitals.shape[0]

    def kernel(s_ref, c_ref, d_ref, g_ref, new_ref, dir_ref):
        total = s_ref[...].sum(axis=0, keepdims=True)
        beta = (total[:, 0:1] - total[:, 1:2]) / total[:, 2:3]
        direction = beta[:, None, None, :] * d_ref[...] - g_ref[...]
        dir_ref[...] = direction
        new_ref[...] = c_ref[...] + step_length * direction

    block = pl.BlockSpec((step,) + orbitals.shape[1:], lambda i: (i, 0, 0, 0))
    out = jax.ShapeDtypeStruct(orbitals.shape, jnp.float32)
    return pl.pallas_call(
        kernel,
        out_shape=(out, out),
        grid=(rows // step,),
        in_specs=[pl.BlockSpec(sums.shape, lambda i: (0, 0)), block, block, block],
        out_specs=(block, block),
        cost_estimate=pl.CostEstimate(flops=4 * orbitals.size, bytes_accessed=20 * orbitals.size, transcendentals=0),
        name="advance",
    )(sums, orbitals, prev_direction, grad)


def on_device(orbitals, potential, prev_gradient, prev_direction):
    own = orbitals.shape[0]
    half = own // 2
    slabs = lax.axis_size("dom")
    c = [orbitals[:half].reshape(half, -1), orbitals[half:].reshape(half, -1)]
    near = gather_near(*c)
    far = gather_far(near)
    image = []
    for index in range(2):
        left = lax.ppermute(c[index], "dom", [(i, i + 1) for i in range(slabs - 1)])
        right = lax.ppermute(c[index], "dom", [(i + 1, i) for i in range(slabs - 1)])
        if index == 0:
            prev, left = lax.optimization_barrier((prev_gradient.reshape(own, -1), left))
        image.append(apply_hamiltonian(c[index], left, right, potential.reshape(1, -1)))
    near_image = gather_near(*image)
    far_image = gather_far(near_image)
    part = gram(c + image, near + far)
    overlap = sum_over_slabs(part)
    grad, sums = gradient_of(
        overlap, near + far, near_image + far_image, image, prev, slabs * c[0].shape[1]
    )
    sums = lax.all_to_all(sums, ("orb", "dom"), split_axis=0, concat_axis=0, tiled=True)
    grad = grad.reshape(orbitals.shape)
    return (*advance(sums, orbitals, prev_direction, grad), grad)


def solution(mesh):
    in_specs = (
        P("orb", "dom", None, None),
        P("dom", None, None),
        P("orb", "dom", None, None),
        P("orb", "dom", None, None),
    )
    out_specs = (
        P("orb", "dom", None, None),
        P("orb", "dom", None, None),
        P("orb", "dom", None, None),
    )
    return jax.shard_map(
        on_device, mesh=mesh, in_specs=in_specs, out_specs=out_specs, check_vma=False
    )
```

```python
import jax
import jax.numpy as jnp
from jax import lax
from jax.experimental import pallas as pl
from jax.experimental.pallas import tpu as pltpu
from jax.sharding import PartitionSpec as P

coeffs = (-205.0 / 72.0, 8.0 / 5.0, -1.0 / 5.0, 8.0 / 315.0, -1.0 / 560.0)
step_length = 0.05
GRAM_VMEM = 56 * 1024 * 1024
GRAM_STRIPS = 4
GRADIENT_STRIPS = 1
GRADIENT_VMEM = 28 * 1024 * 1024
ZS = 8


def shift_orb(v, k):
    n = lax.axis_size("orb")
    return lax.ppermute(v, "orb", [(i, (i + k) % n) for i in range(n)])


def swap_core(v):
    n = lax.axis_size("orb")
    return lax.ppermute(v, "orb", [(i, i ^ 1) for i in range(n)])


def flip_z(v):
    n = lax.axis_size("dom")
    return lax.ppermute(v, "dom", [(i, i ^ 1) for i in range(n)])


def shift_z(v, k):
    n = lax.axis_size("dom")
    return lax.ppermute(v, "dom", [(i, (i // ZS) * ZS + (i + k) % ZS) for i in range(n)])


def shift_y(v, k):
    n = lax.axis_size("dom")
    return lax.ppermute(v, "dom", [(i, (i + k * ZS) % n) for i in range(n)])


def gather_near(first, second):
    right1, left2 = shift_orb(first, 2), shift_orb(second, -2)
    right2, left1 = shift_orb(second, 2), shift_orb(first, -2)
    blocks = [first, second, right1, left2, right2, left1]
    return blocks + [swap_core(b) for b in blocks]


def gather_far(near):
    far1, far2 = shift_orb(near[2], 2), shift_orb(near[3], -2)
    return [far1, far2, swap_core(far1), swap_core(far2)]


def stencil_kernel(c_ref, l_ref, r_ref, v_ref, o_ref):
    lane = lax.broadcasted_iota(jnp.int32, (8, 128), 1)

    @pl.loop(0, c_ref.shape[0] // 8)
    def _(group):
        rows = pl.ds(pl.multiple_of(group * 8, 8), 8)

        def tile(ref, plane, line):
            start = (plane * 8 + line) * 128
            return ref[rows, start : start + 128]

        def plane_tile(plane, line):
            if plane < 0:
                return tile(l_ref, plane + 4, line)
            if plane > 3:
                return tile(r_ref, plane - 4, line)
            return tile(c_ref, plane, line)

        for plane in range(4):
            for line in range(8):
                start = (plane * 8 + line) * 128
                center = tile(c_ref, plane, line)
                total = (v_ref[:, start : start + 128] - 1.5 * coeffs[0]) * center
                for k in range(1, 5):
                    near = plane_tile(plane + k, line) + plane_tile(plane - k, line)
                    if line + k < 8:
                        near = near + tile(c_ref, plane, line + k)
                    if line - k >= 0:
                        near = near + tile(c_ref, plane, line - k)
                    near = near + jnp.where(lane < 128 - k, pltpu.roll(center, 128 - k, 1), 0.0)
                    near = near + jnp.where(lane >= k, pltpu.roll(center, k, 1), 0.0)
                    total = total + (-0.5 * coeffs[k]) * near
                o_ref[rows, start : start + 128] = total


def apply_hamiltonian(c, left, right, pot):
    rows, cells = c.shape
    step = 24
    block = pl.BlockSpec((step, cells), lambda i: (i, 0))
    return pl.pallas_call(
        stencil_kernel,
        out_shape=jax.ShapeDtypeStruct(c.shape, jnp.float32),
        grid=(rows // step,),
        in_specs=[block, block, block, pl.BlockSpec((1, cells), lambda i: (0, 0))],
        out_specs=block,
        cost_estimate=pl.CostEstimate(flops=40 * rows * cells, bytes_accessed=16 * rows * cells, transcendentals=0),
        name="hamiltonian",
    )(c, left, right, pot)


def split(v):
    hi = v.astype(jnp.bfloat16)
    return hi, (v - hi.astype(jnp.float32)).astype(jnp.bfloat16)


def dot_nt(a, b):
    return lax.dot_general(a, b, (((1,), (1,)), ((), ())), preferred_element_type=jnp.float32)


def store_split(refs, hi_ref, lo_ref, columns):
    at = 0
    for ref in refs:
        hi, lo = split(ref[:, columns])
        hi_ref[at : at + ref.shape[0], columns] = hi
        lo_ref[at : at + ref.shape[0], columns] = lo
        at += ref.shape[0]


def strips(chunk, count):
    return [slice(k * chunk // count, (k + 1) * chunk // count) for k in range(count)]


def gram(own_blocks, blocks):
    cells = blocks[0].shape[1]
    count = len(own_blocks)
    rows = sum(b.shape[0] for b in own_blocks)
    total = sum(b.shape[0] for b in blocks)
    chunk = 2048

    def kernel(*rest):
        o_ref, hi_ref, lo_ref, w_ref = rest[-4:]
        part = 0.0
        for strip in strips(chunk, GRAM_STRIPS):
            store_split(rest[count:-4], hi_ref, lo_ref, strip)
            store_split(rest[:count], w_ref.at[0:rows], w_ref.at[rows : 2 * rows], strip)
            with_hi = dot_nt(w_ref[:, strip], hi_ref[:, strip])
            part = part + with_hi[:rows] + with_hi[rows:] + dot_nt(w_ref[0:rows, strip], lo_ref[:, strip])

        @pl.when(pl.program_id(0) == 0)
        def _():
            o_ref[...] = part

        @pl.when(pl.program_id(0) > 0)
        def _():
            o_ref[...] += part

    return pl.pallas_call(
        kernel,
        out_shape=jax.ShapeDtypeStruct((rows, total), jnp.float32),
        grid=(cells // chunk,),
        in_specs=[pl.BlockSpec((b.shape[0], chunk), lambda i: (0, i)) for b in own_blocks + blocks],
        out_specs=pl.BlockSpec((rows, total), lambda i: (0, 0)),
        scratch_shapes=[
            pltpu.VMEM((total, chunk), jnp.bfloat16),
            pltpu.VMEM((total, chunk), jnp.bfloat16),
            pltpu.VMEM((2 * rows, chunk), jnp.bfloat16),
        ],
        compiler_params=pltpu.CompilerParams(vmem_limit_bytes=GRAM_VMEM),
        cost_estimate=pl.CostEstimate(
            flops=6 * rows * total * cells, bytes_accessed=4 * cells * (rows + total), transcendentals=0
        ),
        name="gram",
    )(*own_blocks, *blocks)


def sum_over_slabs(part):
    rows, columns = part.shape
    slabs = lax.axis_size("dom")
    count = slabs // ZS
    dom = lax.axis_index("dom")
    slot = dom // ZS
    even = lax.rem(dom, 2) == 0
    pieces = part.reshape(count, 2, rows // (2 * count), columns)
    quad = ZS // 2

    def piece(k):
        return lax.dynamic_index_in_dim(pieces, lax.rem(slot + k, count), 0, keepdims=False)

    total = piece(0)
    order = sorted(range(1, count), key=lambda k: -min(k, count - k))
    for got in [shift_y(piece(k), k) for k in order]:
        total = total + got
    other = flip_z(jnp.where(even, total[1], total[0]))
    total = jnp.where(even, total[0], total[1]) + other
    for got in [shift_z(total, 2 * k) for k in sorted(range(1, quad), key=lambda k: -min(k, quad - k))]:
        total = total + got
    other = flip_z(total)
    total = jnp.where(even, jnp.stack([total, other]), jnp.stack([other, total]))
    out = jnp.zeros_like(pieces)
    out = lax.dynamic_update_slice_in_dim(out, total[None], slot, 0)
    for k in order:
        out = lax.dynamic_update_slice_in_dim(
            out, shift_y(total, k)[None], lax.rem(slot - k + count, count), 0
        )
    return out.reshape(rows, columns)


def gradient_of(overlap, blocks, images, own_image, prev, cells_total):
    own, cells = prev.shape
    total = overlap.shape[1]
    count = len(blocks)
    devices = lax.axis_size("orb") * lax.axis_size("dom")
    chunk = 1024

    def kernel(s_ref, p_ref, *rest):
        g_ref, sums_ref, w_ref, acc_ref, hi_ref, lo_ref = rest[-6:]
        own_refs, refs = rest[:2], rest[2 : 2 + 2 * count]

        @pl.when(pl.program_id(0) == 0)
        def _():
            for index in range(2):
                hi, lo = split(s_ref[(1 - index) * own : (2 - index) * own, :] * (-2.0 / cells_total))
                w_ref[:own, index * total : (index + 1) * total] = hi
                w_ref[own:, index * total : (index + 1) * total] = lo
            acc_ref[...] = jnp.zeros_like(acc_ref)

        def folded(v):
            v = v.reshape(own // 8, 8, v.shape[1]).sum(0)
            return sum(v[:, k : k + 128] for k in range(0, v.shape[1], 128))

        for strip in strips(chunk, GRADIENT_STRIPS):
            store_split(refs, hi_ref, lo_ref, strip)
            with_hi = jnp.dot(w_ref[...], hi_ref[:, strip], preferred_element_type=jnp.float32)
            grad = with_hi[:own] + with_hi[own:]
            grad = grad + jnp.dot(w_ref[:own, :], lo_ref[:, strip], preferred_element_type=jnp.float32)
            grad = grad + 4.0 * jnp.concatenate([own_refs[0][:, strip], own_refs[1][:, strip]], axis=0)
            g_ref[:, strip] = grad
            prev_block = p_ref[:, strip]
            acc_ref[0:8, :] += folded(grad * grad)
            acc_ref[8:16, :] += folded(grad * prev_block)
            acc_ref[16:24, :] += folded(prev_block * prev_block)

        @pl.when(pl.program_id(0) == cells // chunk - 1)
        def _():
            lane = lax.broadcasted_iota(jnp.int32, (devices, 128), 1)
            row = jnp.zeros((devices, 128), jnp.float32)
            for k in range(3):
                value = acc_ref[8 * k : 8 * k + 8, :].sum(axis=0, keepdims=True).sum(axis=1, keepdims=True)
                row = jnp.where(lane == k, value, row)
            sums_ref[...] = row

    own_block = pl.BlockSpec((own, chunk), lambda i: (0, i))
    column = [pl.BlockSpec((b.shape[0], chunk), lambda i: (0, i)) for b in own_image + blocks + images]
    return pl.pallas_call(
        kernel,
        out_shape=(
            jax.ShapeDtypeStruct((own, cells), jnp.float32),
            jax.ShapeDtypeStruct((devices, 128), jnp.float32),
        ),
        grid=(cells // chunk,),
        in_specs=[pl.BlockSpec((2 * own, total), lambda i: (0, 0)), own_block] + column,
        out_specs=(own_block, pl.BlockSpec((devices, 128), lambda i: (0, 0))),
        scratch_shapes=[
            pltpu.VMEM((2 * own, 2 * total), jnp.bfloat16),
            pltpu.VMEM((24, 128), jnp.float32),
            pltpu.VMEM((2 * total, chunk), jnp.bfloat16),
            pltpu.VMEM((2 * total, chunk), jnp.bfloat16),
        ],
        compiler_params=pltpu.CompilerParams(vmem_limit_bytes=GRADIENT_VMEM),
        cost_estimate=pl.CostEstimate(
            flops=12 * own * total * cells, bytes_accessed=8 * cells * total, transcendentals=0
        ),
        name="gradient",
    )(overlap, prev, *own_image, *blocks, *images)


def advance(sums, orbitals, prev_direction, grad):
    step = 48
    rows = orbitals.shape[0]

    def kernel(s_ref, c_ref, d_ref, g_ref, new_ref, dir_ref):
        total = s_ref[...].sum(axis=0, keepdims=True)
        beta = (total[:, 0:1] - total[:, 1:2]) / total[:, 2:3]
        direction = beta[:, None, None, :] * d_ref[...] - g_ref[...]
        dir_ref[...] = direction
        new_ref[...] = c_ref[...] + step_length * direction

    block = pl.BlockSpec((step,) + orbitals.shape[1:], lambda i: (i, 0, 0, 0))
    out = jax.ShapeDtypeStruct(orbitals.shape, jnp.float32)
    return pl.pallas_call(
        kernel,
        out_shape=(out, out),
        grid=(rows // step,),
        in_specs=[pl.BlockSpec(sums.shape, lambda i: (0, 0)), block, block, block],
        out_specs=(block, block),
        cost_estimate=pl.CostEstimate(flops=4 * orbitals.size, bytes_accessed=20 * orbitals.size, transcendentals=0),
        name="advance",
    )(sums, orbitals, prev_direction, grad)


def on_device(orbitals, potential, prev_gradient, prev_direction):
    own = orbitals.shape[0]
    half = own // 2
    slabs = lax.axis_size("dom")
    c = [orbitals[:half].reshape(half, -1), orbitals[half:].reshape(half, -1)]
    near = gather_near(*c)
    far = gather_far(near)
    image = []
    for index in range(2):
        left = lax.ppermute(c[index], "dom", [(i, i + 1) for i in range(slabs - 1)])
        right = lax.ppermute(c[index], "dom", [(i + 1, i) for i in range(slabs - 1)])
        if index == 0:
            prev, left = lax.optimization_barrier((prev_gradient.reshape(own, -1), left))
        image.append(apply_hamiltonian(c[index], left, right, potential.reshape(1, -1)))
    near_image = gather_near(*image)
    far_image = gather_far(near_image)
    part = gram(c + image, near + far)
    overlap = sum_over_slabs(part)
    grad, sums = gradient_of(
        overlap, near + far, near_image + far_image, image, prev, slabs * c[0].shape[1]
    )
    sums = lax.all_to_all(sums, ("orb", "dom"), split_axis=0, concat_axis=0, tiled=True)
    grad = grad.reshape(orbitals.shape)
    return (*advance(sums, orbitals, prev_direction, grad), grad)


def solution(mesh):
    in_specs = (
        P("orb", "dom", None, None),
        P("dom", None, None),
        P("orb", "dom", None, None),
        P("orb", "dom", None, None),
    )
    out_specs = (
        P("orb", "dom", None, None),
        P("orb", "dom", None, None),
        P("orb", "dom", None, None),
    )
    return jax.shard_map(
        on_device, mesh=mesh, in_specs=in_specs, out_specs=out_specs, check_vma=False
    )
```
